32 devices in a mesh: section: 4 (over z), ctx: 8 (over y, x, core).
Axes of the slice: x: 2, y: 2, z: 4, core: 2. Of those that a mesh axis runs over, the one named last changes fastest.
Arguments:
- stream: bfloat16 [1024, 2688], P('ctx'), may hold values from -6 to 6
- queries: bfloat16 [4, 1024, 2048], P('section', 'ctx'), may hold values from -51 to 51
- keys: bfloat16 [4, 1024, 1024], P('section', 'ctx'), may hold values from -4 to 4
- values: bfloat16 [4, 1024, 1024], P('section', 'ctx'), may hold values from -120 to 120
- out_weight: bfloat16 [4, 2048, 2688], P('section', 'ctx'), may hold values from -0.125 to 0.125
- gains: bfloat16 [4, 2688], P('section'), may hold values from 0.099609375 to 1.8984375
Outputs:
- layer_outputs: bfloat16 [4, 1024, 2688], P('section', 'ctx')
The draws below stay inside these ranges and needn't reach their ends.
All inputs are finite; a program needn't handle non-finite values.
Results may differ from the reference program's by a relative error of at most 0.009.
Values may be sent and summed in bfloat16 or wider, within the bound.
A program may use at most 64 MiB of HBM per device.

```python
import math
import jax
import jax.numpy as jnp
from jax import lax

HQ = 16
KEY_HEADS = 8
HEAD_WIDTH = 128
STREAM_WIDTH = 2688
WINDOW_LENGTH = 1024
QUERY_SCALAR = 168
LAYER_COUNT = 4
TOKEN_COUNT = 1024
QUERY_PER_KEY = 2


def draw_pair(key):
    keys_shape_tuple = (LAYER_COUNT, TOKEN_COUNT, KEY_HEADS * HEAD_WIDTH)
    queries_shape_tuple = (LAYER_COUNT, TOKEN_COUNT, HQ * HEAD_WIDTH)
    sampled_keys = jax.random.truncated_normal(jax.random.fold_in(key, 11), -4.0, 4.0, keys_shape_tuple, jnp.float32)
    drawn_queries = jax.random.truncated_normal(jax.random.fold_in(key, 12), -4.0, 4.0, queries_shape_tuple, jnp.float32)
    return (drawn_queries, sampled_keys)


def draw_queries(key, part):
    return draw_pair(key)[0].astype(jnp.bfloat16)


def draw_keys(key, part):
    return draw_pair(key)[1].astype(jnp.bfloat16)


def draw_values(key, part):
    value_shape_tuple = (LAYER_COUNT, TOKEN_COUNT, KEY_HEADS * HEAD_WIDTH)
    base_draw = jax.random.truncated_normal(jax.random.fold_in(key, 21), -4.0, 4.0, value_shape_tuple, jnp.float32)
    return base_draw.astype(jnp.bfloat16)


def levels(key, dims, shards, smallest, high):
    level = 1.0
    for axis_at, parts in shards:
        heights = jax.random.uniform(jax.random.fold_in(jax.random.fold_in(key, 6), axis_at), (parts,), jnp.float32, smallest / len(shards), high / len(shards))
        level = level * jnp.repeat(jnp.exp(heights), dims[axis_at] // parts).reshape((-1,) + (1,) * (len(dims) - 1 - axis_at))
    return level


def bell_draw(key, shape, width, limit, pieces=(), kind=jnp.bfloat16):
    loudness = levels(key, shape, pieces, -0.22, 0.18) if pieces else 1.0
    array = jax.random.normal(key, shape, jnp.float32) * width * loudness
    return jnp.minimum(jnp.maximum(array, -limit), limit).astype(kind)


def setup_inputs(seed: int = 0) -> dict:
    seeds = jax.random.split(jax.random.key(seed), 7)
    stream = bell_draw(seeds[0], (TOKEN_COUNT, STREAM_WIDTH), 1.0, 6.0, ((0, 8),))
    queries = draw_queries(jax.random.fold_in(seeds[6], 71), 0)
    keys = draw_keys(jax.random.fold_in(seeds[6], 71), 0)
    values = draw_values(jax.random.fold_in(seeds[6], 71), 0)
    out_weight = bell_draw(seeds[4], (LAYER_COUNT, HQ * HEAD_WIDTH, STREAM_WIDTH), (HQ * HEAD_WIDTH) ** -0.5, 0.125, ((0, 4), (1, 8)))
    gains = jnp.clip(1.0 + 0.18 * jax.random.normal(seeds[5], (LAYER_COUNT, STREAM_WIDTH), jnp.float32), 0.099609375, 1.8984375).astype(jnp.bfloat16)
    return dict(stream=stream, queries=queries, keys=keys, values=values, out_weight=out_weight, gains=gains)


norm_eps = 1e-06

def attend_block(query_matrix_rows, key_matrix_rows, value_matrix_rows, allowed, scale_factor):
    scores = jnp.einsum('qhgd,khd->hgqk', query_matrix_rows.astype(jnp.float32), key_matrix_rows.astype(jnp.float32)) * scale_factor
    scores = jnp.where(allowed, scores, -jnp.inf)
    row_top = lax.optimization_barrier(jnp.max(scores, axis=-1, keepdims=True))
    exponent = jnp.exp(scores - row_top)
    row_total = lax.optimization_barrier(jnp.sum(exponent, axis=-1, keepdims=True))
    weights = lax.optimization_barrier(exponent.astype(jnp.bfloat16)).astype(jnp.float32)
    mixed_rows = jnp.einsum('hgqk,khd->qhgd', weights, value_matrix_rows.astype(jnp.float32))
    return mixed_rows / jnp.transpose(row_total, (2, 0, 1, 3))

def attend_layer(queries, keys, values, weight_matrix, gain_row):
    rows_per_block = math.gcd(TOKEN_COUNT, 512)
    block_count = TOKEN_COUNT // rows_per_block
    scale_factor = QUERY_SCALAR ** (-0.5)
    empty_padding_rows = jnp.zeros((WINDOW_LENGTH, KEY_HEADS * HEAD_WIDTH), keys.dtype)
    keys_with_padding = jnp.concatenate([empty_padding_rows, keys], axis=0)
    values_with_padding = jnp.concatenate([empty_padding_rows, values], axis=0)

    def one_block(block_index):
        leading_row = block_index * rows_per_block
        query_matrix_rows = lax.dynamic_slice_in_dim(queries, leading_row, rows_per_block, 0).reshape(rows_per_block, KEY_HEADS, QUERY_PER_KEY, HEAD_WIDTH)
        key_matrix_rows = lax.dynamic_slice_in_dim(keys_with_padding, leading_row, rows_per_block + WINDOW_LENGTH, 0).reshape(rows_per_block + WINDOW_LENGTH, KEY_HEADS, HEAD_WIDTH)
        value_matrix_rows = lax.dynamic_slice_in_dim(values_with_padding, leading_row, rows_per_block + WINDOW_LENGTH, 0).reshape(rows_per_block + WINDOW_LENGTH, KEY_HEADS, HEAD_WIDTH)
        query_pos = leading_row + jnp.arange(rows_per_block, dtype=jnp.int32)
        key_pos = leading_row - WINDOW_LENGTH + jnp.arange(rows_per_block + WINDOW_LENGTH, dtype=jnp.int32)
        allowed = (key_pos[None, :] >= 0) & (key_pos[None, :] <= query_pos[:, None]) & (key_pos[None, :] > query_pos[:, None] - WINDOW_LENGTH)
        mixed_rows = attend_block(query_matrix_rows, key_matrix_rows, value_matrix_rows, allowed, scale_factor)
        attended = mixed_rows.reshape(rows_per_block, HQ * HEAD_WIDTH).astype(jnp.bfloat16)
        return jnp.dot(attended, weight_matrix, preferred_element_type=jnp.float32)
    projected = lax.map(one_block, jnp.arange(block_count, dtype=jnp.int32)).reshape(TOKEN_COUNT, STREAM_WIDTH)
    mean_square = lax.optimization_barrier(jnp.mean(projected * projected, axis=-1, keepdims=True))
    return projected * lax.rsqrt(mean_square + norm_eps) * gain_row.astype(jnp.float32)

def reference(stream, queries, keys, values, out_weight, gains):
    running = stream.astype(jnp.float32)
    outputs_list = []
    for layer_index in range(LAYER_COUNT):
        branch = attend_layer(queries[layer_index], keys[layer_index], values[layer_index], out_weight[layer_index], gains[layer_index])
        running = running + branch
        outputs_list.append(running.astype(jnp.bfloat16))
    return jnp.stack(outputs_list)
```

```python
import functools
import math

import jax
import jax.numpy as jnp
from jax import lax
from jax.experimental import pallas as pl
from jax.experimental.pallas import tpu as pltpu
from jax.sharding import PartitionSpec as P

KEY_HEADS = 8
HEAD_WIDTH = 128
WINDOW_LENGTH = 1024
QUERY_SCALAR = 168
QUERY_PER_KEY = 2


norm_eps = 1e-06


def passed_along(block, axis, distance):
    devices = range(lax.axis_size(axis))
    route = [(i - distance, i) for i in devices if i - distance in devices]
    return lax.ppermute(block, axis, route)


def attend_block(query_matrix_rows, key_matrix_rows, value_matrix_rows, allowed, scale_factor):
    scores = (
        jnp.einsum(
            "qhgd,khd->hgqk", query_matrix_rows, key_matrix_rows, preferred_element_type=jnp.float32
        )
        * scale_factor
    )
    scores = jnp.where(allowed, scores, -jnp.inf)
    row_top = jnp.max(scores, axis=-1, keepdims=True)
    exponent = jnp.exp(scores - row_top)
    row_total = jnp.sum(exponent, axis=-1, keepdims=True)
    weights = exponent.astype(jnp.bfloat16)
    mixed_rows = jnp.einsum(
        "hgqk,khd->qhgd", weights, value_matrix_rows, preferred_element_type=jnp.float32
    )
    return mixed_rows / jnp.transpose(row_total, (2, 0, 1, 3))


def local(stream, queries, keys, values, out_weight, gains):
    tok_rows = stream.shape[0]
    span_rows = min(tok_rows, WINDOW_LENGTH)
    hop_count = WINDOW_LENGTH // span_rows
    own_tail = (keys[0, tok_rows - span_rows :], values[0, tok_rows - span_rows :])
    pieces = [
        passed_along((own_tail[0], own_tail[1]), "ctx", distance)
        for distance in range(hop_count, 0, -1)
    ]
    key_matrix_rows = jnp.concatenate([piece_pair[0] for piece_pair in pieces] + [keys[0]], axis=0)
    value_matrix_rows = jnp.concatenate(
        [piece_pair[1] for piece_pair in pieces] + [values[0]], axis=0
    )
    ctx_base = lax.axis_index("ctx") * tok_rows
    query_pos = ctx_base + jnp.arange(tok_rows, dtype=jnp.int32)
    key_pos = ctx_base - WINDOW_LENGTH + jnp.arange(WINDOW_LENGTH + tok_rows, dtype=jnp.int32)
    allowed = (
        (key_pos[None, :] >= 0)
        & (key_pos[None, :] <= query_pos[:, None])
        & (key_pos[None, :] > query_pos[:, None] - WINDOW_LENGTH)
    )
    scale_factor = QUERY_SCALAR ** (-0.5)
    heads_per_block = math.gcd(KEY_HEADS, 4)
    query_width = heads_per_block * QUERY_PER_KEY * HEAD_WIDTH
    key_width = heads_per_block * HEAD_WIDTH
    outputs_list = []
    for query_head_group in range(KEY_HEADS // heads_per_block):
        query_cols = queries[
            0, :, query_head_group * query_width : (query_head_group + 1) * query_width
        ].reshape(tok_rows, heads_per_block, QUERY_PER_KEY, HEAD_WIDTH)
        key_cols = key_matrix_rows[
            :, query_head_group * key_width : (query_head_group + 1) * key_width
        ].reshape(WINDOW_LENGTH + tok_rows, heads_per_block, HEAD_WIDTH)
        value_cols = value_matrix_rows[
            :, query_head_group * key_width : (query_head_group + 1) * key_width
        ].reshape(WINDOW_LENGTH + tok_rows, heads_per_block, HEAD_WIDTH)
        mixed_rows = attend_block(query_cols, key_cols, value_cols, allowed, scale_factor)
        outputs_list.append(mixed_rows.reshape(tok_rows, query_width))
    attended = jnp.concatenate(outputs_list, axis=1).astype(jnp.bfloat16)
    projected = jnp.dot(
        attended,
        lax.all_gather(out_weight[0], "ctx", axis=0, tiled=True),
        preferred_element_type=jnp.float32,
    )
    mean_square = jnp.mean(projected * projected, axis=-1, keepdims=True)
    branch = projected * lax.rsqrt(mean_square + norm_eps) * gains[0].astype(jnp.float32)
    section_index = lax.axis_index("section")
    section_count = lax.axis_size("section")
    running = jnp.where(
        section_index == 0, stream.astype(jnp.float32) + branch, jnp.zeros_like(branch)
    )
    for turn_index in range(section_count - 1):
        arrived = passed_along(running.astype(jnp.bfloat16), "section", 1).astype(running.dtype)
        running = jnp.where(section_index == turn_index + 1, arrived + branch, running)
    return running.astype(jnp.bfloat16)[None]


LANES = 128
MESH = pl.DeviceIdType.MESH
CHUNKS = 4


def column_tiles(start, stop, width):
    return [(at, min(at + width, stop) - at) for at in range(start, stop, width)]


def fused_kernel(
    sections,
    chunks,
    half,
    gains_ref,
    stream_ref,
    q_ref,
    k_ref,
    v_ref,
    w_hbm,
    out_ref,
    qbuf,
    kbuf,
    vbuf,
    w_ref,
    att,
    pair_out,
    pair_in,
    x1_out,
    x1_in,
    y1_out,
    y1_in,
    x2_out,
    x2_in,
    y2_out,
    y2_in,
    keep_me,
    keep_x,
    keep_y,
    base,
    local_sem,
    a2a_send,
    a2a_recv,
    pair_sem,
    x1_sem,
    y1_sem,
    x2_sem,
    y2_sem,
    chain_sem,
):
    me = lax.axis_index("ctx")
    section = lax.axis_index("section")
    devices, rows, query_width = qbuf.shape
    width = w_ref.shape[1]
    chunk_rows = rows // chunks
    quarter, pair_count = devices // 4, devices // 2
    core = me % 2
    across = (me // quarter) % 2
    up = me // pair_count
    flips = (1 - 2 * core, quarter * (1 - 2 * across), pair_count * (1 - 2 * up))

    def peer(flip_core, flip_x, flip_y):
        return me + flips[0] * flip_core + flips[1] * flip_x + flips[2] * flip_y

    sibling, beside, above, diagonal = peer(1, 0, 0), peer(0, 1, 0), peer(0, 0, 1), peer(0, 1, 1)
    has_prev = jnp.minimum(section, 1)
    has_next = jnp.minimum(sections - 1 - section, 1)

    def own_rows(buf):
        return buf.at[pl.ds(pl.multiple_of(me * rows, rows), rows)]

    def head_columns(ref, who, span):
        return ref.at[:, pl.ds(pl.multiple_of(who * span, span), span)]

    w_copy = pltpu.make_async_copy(w_hbm, w_ref, local_sem.at[0])
    w_copy.start()

    @pl.when(section == 0)
    def _():
        for chunk in range(chunks):
            pltpu.make_async_copy(
                stream_ref.at[pl.ds(chunk * chunk_rows, chunk_rows)],
                base.at[chunk],
                chain_sem.at[1, chunk],
            ).start()

    own = [
        (head_columns(q_ref, me, query_width), qbuf.at[me], 0),
        (head_columns(k_ref, me, HEAD_WIDTH), own_rows(kbuf), 1),
        (head_columns(v_ref, me, HEAD_WIDTH), own_rows(vbuf), 2),
    ]
    for source, target, which in own:
        pltpu.make_async_copy(source, target, a2a_recv.at[which, me]).start()

    order = [(0, 1, 1), (1, 1, 1), (0, 1, 0), (0, 0, 1), (1, 1, 0), (1, 0, 1), (1, 0, 0)]
    barrier = pltpu.get_barrier_semaphore()
    for flip in order:
        pl.semaphore_signal(barrier, inc=1, device_id=(section, peer(*flip)), device_id_type=MESH)

    @pl.when(section > 0)
    def _():
        pl.semaphore_signal(barrier, inc=1, device_id=(section - 1, me), device_id_type=MESH)

    @pl.when(section < sections - 1)
    def _():
        pl.semaphore_signal(barrier, inc=1, device_id=(section + 1, me), device_id_type=MESH)

    pl.semaphore_wait(barrier, len(order) + has_prev + has_next)

    def exchange(who):
        return [
            pltpu.make_async_remote_copy(
                src_ref=source,
                dst_ref=target,
                send_sem=a2a_send.at[which, who],
                recv_sem=a2a_recv.at[which, me],
                device_id=(section, who),
                device_id_type=MESH,
            )
            for source, target, which in (
                (head_columns(k_ref, who, HEAD_WIDTH), own_rows(kbuf), 1),
                (head_columns(v_ref, who, HEAD_WIDTH), own_rows(vbuf), 2),
                (head_columns(q_ref, who, query_width), qbuf.at[me], 0),
            )
        ]

    for flip in order:
        for copy in exchange(peer(*flip)):
            copy.start()

    def arrive(block):
        for which, target in (
            (0, qbuf.at[block]),
            (1, kbuf.at[pl.ds(block * rows, rows)]),
            (2, vbuf.at[pl.ds(block * rows, rows)]),
        ):
            pltpu.make_async_copy(target, target, a2a_recv.at[which, block]).wait()

    factor = QUERY_SCALAR ** (-0.5) * math.log2(math.e)
    seen = lax.broadcasted_iota(jnp.int32, (rows, rows), 1) <= lax.broadcasted_iota(
        jnp.int32, (rows, rows), 0
    )
    for block in range(devices):
        arrive(block)
        reach = (block + 1) * rows
        for head in range(query_width // HEAD_WIDTH):
            columns = slice(head * HEAD_WIDTH, (head + 1) * HEAD_WIDTH)
            scores = lax.dot_general(
                qbuf[block, :, columns],
                kbuf[0:reach],
                (((1,), (1,)), ((), ())),
                preferred_element_type=jnp.float32,
            )
            last = jnp.where(seen, scores[:, block * rows :], -jnp.inf)
            if block:
                scores = jnp.concatenate([scores[:, : block * rows], last], axis=1)
            else:
                scores = last
            top = jnp.max(scores, axis=1, keepdims=True)
            exponent = jnp.exp2((scores - top) * factor)
            total = jnp.sum(exponent, axis=1, keepdims=True)
            mixed = jnp.dot(
                exponent.astype(jnp.bfloat16), vbuf[0:reach], preferred_element_type=jnp.float32
            )
            mixed = (mixed / total).astype(jnp.bfloat16)
            for chunk in range(chunks):
                att[block % 2, chunk, block // 2, :, columns] = mixed[
                    chunk * chunk_rows : (chunk + 1) * chunk_rows
                ]

    w_copy.wait()

    def remote(source, target, sems, chunk, who):
        return pltpu.make_async_remote_copy(
            src_ref=source.at[chunk],
            dst_ref=target.at[chunk],
            send_sem=sems.at[0, chunk],
            recv_sem=sems.at[1, chunk],
            device_id=who,
            device_id_type=MESH,
        )

    def pair_copy(chunk):
        return remote(pair_out, pair_in, pair_sem, chunk, (section, sibling))

    def x1_copy(chunk):
        return remote(x1_out, x1_in, x1_sem, chunk, (section, beside))

    def y1_copy(chunk):
        return remote(y1_out, y1_in, y1_sem, chunk, (section, above))

    def x2_copy(chunk):
        return remote(x2_out, x2_in, x2_sem, chunk, (section, beside))

    def y2_copy(chunk):
        return remote(y2_out, y2_in, y2_sem, chunk, (section, above))

    def chain_copy(chunk):
        return pltpu.make_async_remote_copy(
            src_ref=out_ref.at[chunk],
            dst_ref=base.at[chunk],
            send_sem=chain_sem.at[0, chunk],
            recv_sem=chain_sem.at[1, chunk],
            device_id=(jnp.minimum(section + 1, sections - 1), me),
            device_id_type=MESH,
        )

    chip_count = pair_count
    places = [who // 2 for who in (beside, diagonal, above, me)]

    def for_sibling(chunk):
        left = att[1 - core, chunk].reshape(chip_count * chunk_rows, query_width)
        for at, span in column_tiles(0, width, 512):
            part = jnp.dot(left, w_ref[:, at : at + span], preferred_element_type=jnp.float32)
            pair_out[chunk, :, :, at : at + span] = part.astype(jnp.bfloat16).reshape(
                chip_count, chunk_rows, span
            )
        pair_copy(chunk).start()

    def first_turn(chunk):
        pair_copy(chunk).wait_recv()
        left = jnp.concatenate([att[core, chunk, place] for place in places], axis=0)

        def summed(at, span):
            part = jnp.dot(left, w_ref[:, at : at + span], preferred_element_type=jnp.float32)
            return [
                part[index * chunk_rows : (index + 1) * chunk_rows]
                + pair_in[chunk, place, :, at : at + span].astype(jnp.float32)
                for index, place in enumerate(places)
            ]

        for at, span in column_tiles(0, half, 512):
            to_beside, to_diagonal, to_above, mine = summed(at, span)
            x1_out[chunk, 0, :, at : at + span] = to_beside.astype(jnp.bfloat16)
            x1_out[chunk, 1, :, at : at + span] = to_diagonal.astype(jnp.bfloat16)
            keep_y[chunk, :, at : at + span] = to_above
            keep_me[chunk, :, at : at + span] = mine
        x1_copy(chunk).start()
        for at, span in column_tiles(half, width, 512):
            to_beside, to_diagonal, to_above, mine = summed(at, span)
            y1_out[chunk, 0, :, at - half : at - half + span] = to_above.astype(jnp.bfloat16)
            y1_out[chunk, 1, :, at - half : at - half + span] = to_diagonal.astype(jnp.bfloat16)
            keep_x[chunk, :, at - half : at - half + span] = to_beside
            keep_me[chunk, :, at : at + span] = mine
        y1_copy(chunk).start()

    def second_turn(chunk):
        x1_copy(chunk).wait_recv()
        y2_out[chunk] = (keep_y[chunk] + x1_in[chunk, 1].astype(jnp.float32)).astype(jnp.bfloat16)
        y2_copy(chunk).start()
        y1_copy(chunk).wait_recv()
        x2_out[chunk] = (keep_x[chunk] + y1_in[chunk, 1].astype(jnp.float32)).astype(jnp.bfloat16)
        x2_copy(chunk).start()
        keep_me[chunk, :, :half] += x1_in[chunk, 0].astype(jnp.float32)
        keep_me[chunk, :, half:] += y1_in[chunk, 0].astype(jnp.float32)

    def normalise(chunk):
        y2_copy(chunk).wait_recv()
        x2_copy(chunk).wait_recv()
        low = keep_me[chunk, :, :half] + y2_in[chunk].astype(jnp.float32)
        high = keep_me[chunk, :, half:] + x2_in[chunk].astype(jnp.float32)
        squares = jnp.sum(low * low, axis=1, keepdims=True) + jnp.sum(
            high * high, axis=1, keepdims=True
        )
        ratio = lax.rsqrt(squares * (1.0 / width) + norm_eps)
        keep_me[chunk, :, :half] = low * ratio * gains_ref[:, :half].astype(jnp.float32)
        keep_me[chunk, :, half:] = high * ratio * gains_ref[:, half:].astype(jnp.float32)

    def hand_on(chunk):
        pltpu.make_async_copy(base.at[chunk], base.at[chunk], chain_sem.at[1, chunk]).wait()
        out_ref[chunk] = (base[chunk].astype(jnp.float32) + keep_me[chunk]).astype(out_ref.dtype)

        @pl.when(section < sections - 1)
        def _():
            chain_copy(chunk).start()

    def turn(step, carry):
        for lag, stage in enumerate((for_sibling, first_turn, second_turn, normalise)):
            chunk = step - lag

            @pl.when((chunk >= 0) & (chunk < chunks))
            def _():
                stage(chunk)

        passed = step - 3 - section

        @pl.when((passed >= 0) & (passed < chunks))
        def _():
            hand_on(passed)

        return carry

    lax.fori_loop(0, chunks + 3 + sections - 1, turn, 0)

    for flip in order:
        for copy in exchange(peer(*flip)):
            copy.wait_send()

    def finish(chunk, carry):
        for copy in (pair_copy, x1_copy, y1_copy, x2_copy, y2_copy):
            copy(chunk).wait_send()

        @pl.when(section < sections - 1)
        def _():
            chain_copy(chunk).wait_send()

        return carry

    lax.fori_loop(0, chunks, finish, 0)


def by_head(sections, chunks, stream, queries, keys, values, out_weight, gains):
    devices = lax.axis_size("ctx")
    rows, width = stream.shape
    query_width = queries.shape[2] // devices
    chunk_rows = rows // chunks
    half = (width // LANES + 1) // 2 * LANES
    other = width - half
    chips = devices // 2
    narrow, wide = jnp.bfloat16, jnp.float32
    anywhere = pl.BlockSpec(memory_space=pl.ANY)
    in_vmem = pl.BlockSpec(memory_space=pltpu.VMEM)
    dma = pltpu.SemaphoreType.DMA
    out = pl.pallas_call(
        functools.partial(fused_kernel, sections, chunks, half),
        out_shape=jax.ShapeDtypeStruct((chunks, chunk_rows, width), narrow),
        in_specs=[in_vmem] + [anywhere] * 5,
        out_specs=in_vmem,
        scratch_shapes=[
            pltpu.VMEM((devices, rows, query_width), narrow),
            pltpu.VMEM((devices * rows, HEAD_WIDTH), narrow),
            pltpu.VMEM((devices * rows, HEAD_WIDTH), narrow),
            pltpu.VMEM(out_weight.shape[1:], narrow),
            pltpu.VMEM((2, chunks, chips, chunk_rows, query_width), narrow),
            pltpu.VMEM((chunks, chips, chunk_rows, width), narrow),
            pltpu.VMEM((chunks, chips, chunk_rows, width), narrow),
            pltpu.VMEM((chunks, 2, chunk_rows, half), narrow),
            pltpu.VMEM((chunks, 2, chunk_rows, half), narrow),
            pltpu.VMEM((chunks, 2, chunk_rows, other), narrow),
            pltpu.VMEM((chunks, 2, chunk_rows, other), narrow),
            pltpu.VMEM((chunks, chunk_rows, other), narrow),
            pltpu.VMEM((chunks, chunk_rows, other), narrow),
            pltpu.VMEM((chunks, chunk_rows, half), narrow),
            pltpu.VMEM((chunks, chunk_rows, half), narrow),
            pltpu.VMEM((chunks, chunk_rows, width), wide),
            pltpu.VMEM((chunks, chunk_rows, other), wide),
            pltpu.VMEM((chunks, chunk_rows, half), wide),
            pltpu.VMEM((chunks, chunk_rows, width), narrow),
            dma((1,)),
            dma((3, devices)),
            dma((3, devices)),
            dma((2, chunks)),
            dma((2, chunks)),
            dma((2, chunks)),
            dma((2, chunks)),
            dma((2, chunks)),
            dma((2, chunks)),
        ],
        compiler_params=pltpu.CompilerParams(
            collective_id=0, has_side_effects=True, vmem_limit_bytes=48 * 1024 * 1024
        ),
    )(gains, stream, queries[0], keys[0], values[0], out_weight[0])
    return out.reshape(1, rows, width)


def fits_by_head(mesh, rows):
    devices = mesh.shape["ctx"]
    return devices == KEY_HEADS and devices * rows <= WINDOW_LENGTH and devices % 8 == 0


def solution(mesh):
    in_specs = (
        P("ctx", None),
        P("section", "ctx", None),
        P("section", "ctx", None),
        P("section", "ctx", None),
        P("section", "ctx", None),
        P("section", None),
    )
    out_specs = P("section", "ctx", None)
    sections = mesh.shape["section"]

    def step(stream, *rest):
        rows = stream.shape[0]
        if fits_by_head(mesh, rows):
            return by_head(sections, CHUNKS, stream, *rest)
        return local(stream, *rest)

    return jax.shard_map(step, mesh=mesh, in_specs=in_specs, out_specs=out_specs, check_vma=False)
```

```python
import functools
import math

import jax
import jax.numpy as jnp
from jax import lax
from jax.experimental import pallas as pl
from jax.experimental.pallas import tpu as pltpu
from jax.sharding import PartitionSpec as P

KEY_HEADS = 8
HEAD_WIDTH = 128
WINDOW_LENGTH = 1024
QUERY_SCALAR = 168
QUERY_PER_KEY = 2


norm_eps = 1e-06


def passed_along(block, axis, distance):
    devices = range(lax.axis_size(axis))
    route = [(i - distance, i) for i in devices if i - distance in devices]
    return lax.ppermute(block, axis, route)


def attend_block(query_matrix_rows, key_matrix_rows, value_matrix_rows, allowed, scale_factor):
    scores = (
        jnp.einsum(
            "qhgd,khd->hgqk", query_matrix_rows, key_matrix_rows, preferred_element_type=jnp.float32
        )
        * scale_factor
    )
    scores = jnp.where(allowed, scores, -jnp.inf)
    row_top = jnp.max(scores, axis=-1, keepdims=True)
    exponent = jnp.exp(scores - row_top)
    row_total = jnp.sum(exponent, axis=-1, keepdims=True)
    weights = exponent.astype(jnp.bfloat16)
    mixed_rows = jnp.einsum(
        "hgqk,khd->qhgd", weights, value_matrix_rows, preferred_element_type=jnp.float32
    )
    return mixed_rows / jnp.transpose(row_total, (2, 0, 1, 3))


def local(stream, queries, keys, values, out_weight, gains):
    tok_rows = stream.shape[0]
    span_rows = min(tok_rows, WINDOW_LENGTH)
    hop_count = WINDOW_LENGTH // span_rows
    own_tail = (keys[0, tok_rows - span_rows :], values[0, tok_rows - span_rows :])
    pieces = [
        passed_along((own_tail[0], own_tail[1]), "ctx", distance)
        for distance in range(hop_count, 0, -1)
    ]
    key_matrix_rows = jnp.concatenate([piece_pair[0] for piece_pair in pieces] + [keys[0]], axis=0)
    value_matrix_rows = jnp.concatenate(
        [piece_pair[1] for piece_pair in pieces] + [values[0]], axis=0
    )
    ctx_base = lax.axis_index("ctx") * tok_rows
    query_pos = ctx_base + jnp.arange(tok_rows, dtype=jnp.int32)
    key_pos = ctx_base - WINDOW_LENGTH + jnp.arange(WINDOW_LENGTH + tok_rows, dtype=jnp.int32)
    allowed = (
        (key_pos[None, :] >= 0)
        & (key_pos[None, :] <= query_pos[:, None])
        & (key_pos[None, :] > query_pos[:, None] - WINDOW_LENGTH)
    )
    scale_factor = QUERY_SCALAR ** (-0.5)
    heads_per_block = math.gcd(KEY_HEADS, 4)
    query_width = heads_per_block * QUERY_PER_KEY * HEAD_WIDTH
    key_width = heads_per_block * HEAD_WIDTH
    outputs_list = []
    for query_head_group in range(KEY_HEADS // heads_per_block):
        query_cols = queries[
            0, :, query_head_group * query_width : (query_head_group + 1) * query_width
        ].reshape(tok_rows, heads_per_block, QUERY_PER_KEY, HEAD_WIDTH)
        key_cols = key_matrix_rows[
            :, query_head_group * key_width : (query_head_group + 1) * key_width
        ].reshape(WINDOW_LENGTH + tok_rows, heads_per_block, HEAD_WIDTH)
        value_cols = value_matrix_rows[
            :, query_head_group * key_width : (query_head_group + 1) * key_width
        ].reshape(WINDOW_LENGTH + tok_rows, heads_per_block, HEAD_WIDTH)
        mixed_rows = attend_block(query_cols, key_cols, value_cols, allowed, scale_factor)
        outputs_list.append(mixed_rows.reshape(tok_rows, query_width))
    attended = jnp.concatenate(outputs_list, axis=1).astype(jnp.bfloat16)
    projected = jnp.dot(
        attended,
        lax.all_gather(out_weight[0], "ctx", axis=0, tiled=True),
        preferred_element_type=jnp.float32,
    )
    mean_square = jnp.mean(projected * projected, axis=-1, keepdims=True)
    branch = projected * lax.rsqrt(mean_square + norm_eps) * gains[0].astype(jnp.float32)
    section_index = lax.axis_index("section")
    section_count = lax.axis_size("section")
    running = jnp.where(
        section_index == 0, stream.astype(jnp.float32) + branch, jnp.zeros_like(branch)
    )
    for turn_index in range(section_count - 1):
        arrived = passed_along(running.astype(jnp.bfloat16), "section", 1).astype(running.dtype)
        running = jnp.where(section_index == turn_index + 1, arrived + branch, running)
    return running.astype(jnp.bfloat16)[None]


LANES = 128
MESH = pl.DeviceIdType.MESH
CHUNKS = 8
PARTS = 2
LEAD = 2
VMEM_GRANT = 66_300_000


def column_tiles(start, stop, width):
    return [(at, min(at + width, stop) - at) for at in range(start, stop, width)]


def fused_kernel(
    sections,
    chunks,
    parts,
    half,
    gains_hbm,
    stream_ref,
    q_ref,
    k_ref,
    v_ref,
    w_hbm,
    out_ref,
    qbuf,
    kbuf,
    vbuf,
    w_ref,
    gains_ref,
    att,
    pair_out,
    pair_in,
    x1_out,
    x1_in,
    y1_out,
    y1_in,
    x2_out,
    x2_in,
    y2_out,
    y2_in,
    keep_me,
    keep_x,
    keep_y,
    base,
    local_sem,
    a2a_send,
    a2a_recv,
    pair_sem,
    x1_sem,
    y1_sem,
    x2_sem,
    y2_sem,
    chain_sem,
):
    me = lax.axis_index("ctx")
    section = lax.axis_index("section")
    devices, rows, query_width = qbuf.shape
    width = w_ref.shape[1]
    chunk_rows = rows // chunks
    quarter, pair_count = devices // 4, devices // 2
    core = me % 2
    across = (me // quarter) % 2
    up = me // pair_count
    flips = (1 - 2 * core, quarter * (1 - 2 * across), pair_count * (1 - 2 * up))

    def peer(flip_core, flip_x, flip_y):
        return me + flips[0] * flip_core + flips[1] * flip_x + flips[2] * flip_y

    sibling, beside, above, diagonal = peer(1, 0, 0), peer(0, 1, 0), peer(0, 0, 1), peer(0, 1, 1)
    has_prev = jnp.minimum(section, 1)
    has_next = jnp.minimum(sections - 1 - section, 1)

    def own_rows(buf):
        return buf.at[pl.ds(pl.multiple_of(me * rows, rows), rows)]

    def head_columns(ref, who, span):
        return ref.at[:, pl.ds(pl.multiple_of(who * span, span), span)]

    w_copy = pltpu.make_async_copy(w_hbm, w_ref, local_sem.at[0])
    w_copy.start()
    gains_copy = pltpu.make_async_copy(gains_hbm, gains_ref, local_sem.at[1])
    gains_copy.start()

    @pl.when(section == 0)
    def _():
        for chunk in range(chunks):
            pltpu.make_async_copy(
                stream_ref.at[pl.ds(chunk * chunk_rows, chunk_rows)],
                base.at[chunk],
                chain_sem.at[1, chunk],
            ).start()

    part_rows = rows // parts

    def query_part(who, part):
        source = q_ref.at[
            pl.ds(part * part_rows, part_rows),
            pl.ds(pl.multiple_of(who * query_width, query_width), query_width),
        ]
        return source, qbuf.at[me, pl.ds(part * part_rows, part_rows)]

    def pieces(who):
        return [
            (head_columns(k_ref, who, HEAD_WIDTH), own_rows(kbuf)),
            (head_columns(v_ref, who, HEAD_WIDTH), own_rows(vbuf)),
        ] + [query_part(who, part) for part in range(parts)]

    for which, (source, target) in enumerate(pieces(me)):
        pltpu.make_async_copy(source, target, a2a_recv.at[which, me]).start()

    order = [(0, 1, 1), (1, 1, 1), (0, 1, 0), (0, 0, 1), (1, 1, 0), (1, 0, 1), (1, 0, 0)]
    barrier = pltpu.get_barrier_semaphore()
    for flip in order:
        pl.semaphore_signal(barrier, inc=1, device_id=(section, peer(*flip)), device_id_type=MESH)

    @pl.when(section > 0)
    def _():
        pl.semaphore_signal(barrier, inc=1, device_id=(section - 1, me), device_id_type=MESH)

    @pl.when(section < sections - 1)
    def _():
        pl.semaphore_signal(barrier, inc=1, device_id=(section + 1, me), device_id_type=MESH)

    pl.semaphore_wait(barrier, len(order) + has_prev + has_next)

    def exchange(who):
        return [
            pltpu.make_async_remote_copy(
                src_ref=source,
                dst_ref=target,
                send_sem=a2a_send.at[which, who],
                recv_sem=a2a_recv.at[which, me],
                device_id=(section, who),
                device_id_type=MESH,
            )
            for which, (source, target) in enumerate(pieces(who))
        ]

    exchanges = [exchange(peer(*flip)) for flip in order]
    for wave in zip(*exchanges):
        for copy in wave:
            copy.start()

    def arrive(which, target, block):
        pltpu.make_async_copy(target, target, a2a_recv.at[which, block]).wait()

    factor = QUERY_SCALAR ** (-0.5) * math.log2(math.e)
    group = query_width // HEAD_WIDTH
    part_chunks = chunks // parts

    def attend(part):
        low = pl.multiple_of(part * part_rows, part_rows)
        place = lax.broadcasted_iota(jnp.int32, (group, part_rows, rows), 1) + low
        seen = lax.broadcasted_iota(jnp.int32, (group, part_rows, rows), 2) <= place
        seen = seen.reshape(group * part_rows, rows)
        for block in range(devices):

            @pl.when(part == 0)
            def _():
                arrive(0, kbuf.at[pl.ds(block * rows, rows)], block)
                arrive(1, vbuf.at[pl.ds(block * rows, rows)], block)

            arrive(2 + part, qbuf.at[block, pl.ds(low, part_rows)], block)
            reach = (block + 1) * rows
            asked = jnp.concatenate(
                [
                    qbuf[block, pl.ds(low, part_rows), head * HEAD_WIDTH : (head + 1) * HEAD_WIDTH]
                    for head in range(group)
                ],
                axis=0,
            )
            scores = lax.dot_general(
                asked,
                kbuf[0:reach],
                (((1,), (1,)), ((), ())),
                preferred_element_type=jnp.float32,
            )
            last = jnp.where(seen, scores[:, block * rows :], -jnp.inf)
            if block:
                scores = jnp.concatenate([scores[:, : block * rows], last], axis=1)
            else:
                scores = last
            top = jnp.max(scores, axis=1, keepdims=True)
            exponent = jnp.exp2((scores - top) * factor)
            total = jnp.sum(exponent, axis=1, keepdims=True)
            mixed = jnp.dot(
                exponent.astype(jnp.bfloat16), vbuf[0:reach], preferred_element_type=jnp.float32
            )
            mixed = (mixed / total).astype(jnp.bfloat16)
            for head in range(group):
                for chunk in range(part_chunks):
                    start = head * part_rows + chunk * chunk_rows
                    att[
                        block % 2,
                        part * part_chunks + chunk,
                        block // 2,
                        :,
                        head * HEAD_WIDTH : (head + 1) * HEAD_WIDTH,
                    ] = mixed[start : start + chunk_rows]

    def remote(source, target, sems, chunk, who):
        return pltpu.make_async_remote_copy(
            src_ref=source.at[chunk],
            dst_ref=target.at[chunk],
            send_sem=sems.at[0, chunk],
            recv_sem=sems.at[1, chunk],
            device_id=who,
            device_id_type=MESH,
        )

    def pair_copy(chunk):
        return remote(pair_out, pair_in, pair_sem, chunk, (section, sibling))

    def x1_copy(chunk):
        return remote(x1_out, x1_in, x1_sem, chunk, (section, beside))

    def y1_copy(chunk):
        return remote(y1_out, y1_in, y1_sem, chunk, (section, above))

    def x2_copy(chunk):
        return remote(x2_out, x2_in, x2_sem, chunk, (section, beside))

    def y2_copy(chunk):
        return remote(y2_out, y2_in, y2_sem, chunk, (section, above))

    def chain_copy(chunk):
        return pltpu.make_async_remote_copy(
            src_ref=out_ref.at[chunk],
            dst_ref=base.at[chunk],
            send_sem=chain_sem.at[0, chunk],
            recv_sem=chain_sem.at[1, chunk],
            device_id=(jnp.minimum(section + 1, sections - 1), me),
            device_id_type=MESH,
        )

    chip_count = pair_count
    places = [who // 2 for who in (beside, diagonal, above, me)]

    def for_sibling(chunk):
        left = att[1 - core, chunk].reshape(chip_count * chunk_rows, query_width)
        for at, span in column_tiles(0, width, 512):
            part = jnp.dot(left, w_ref[:, at : at + span], preferred_element_type=jnp.float32)
            pair_out[chunk, :, :, at : at + span] = part.astype(jnp.bfloat16).reshape(
                chip_count, chunk_rows, span
            )
        pair_copy(chunk).start()

    def first_turn(chunk):
        pair_copy(chunk).wait_recv()
        left = jnp.concatenate([att[core, chunk, place] for place in places], axis=0)

        def summed(at, span):
            part = jnp.dot(left, w_ref[:, at : at + span], preferred_element_type=jnp.float32)
            return [
                part[index * chunk_rows : (index + 1) * chunk_rows]
                + pair_in[chunk, place, :, at : at + span].astype(jnp.float32)
                for index, place in enumerate(places)
            ]

        for at, span in column_tiles(0, half, 512):
            to_beside, to_diagonal, to_above, mine = summed(at, span)
            x1_out[chunk, 0, :, at : at + span] = to_beside.astype(jnp.bfloat16)
            x1_out[chunk, 1, :, at : at + span] = to_diagonal.astype(jnp.bfloat16)
            keep_y[chunk, :, at : at + span] = to_above
            keep_me[chunk, :, at : at + span] = mine
        x1_copy(chunk).start()
        for at, span in column_tiles(half, width, 512):
            to_beside, to_diagonal, to_above, mine = summed(at, span)
            y1_out[chunk, 0, :, at - half : at - half + span] = to_above.astype(jnp.bfloat16)
            y1_out[chunk, 1, :, at - half : at - half + span] = to_diagonal.astype(jnp.bfloat16)
            keep_x[chunk, :, at - half : at - half + span] = to_beside
            keep_me[chunk, :, at : at + span] = mine
        y1_copy(chunk).start()

    def second_turn(chunk):
        x1_copy(chunk).wait_recv()
        y2_out[chunk] = (keep_y[chunk] + x1_in[chunk, 1].astype(jnp.float32)).astype(jnp.bfloat16)
        y2_copy(chunk).start()
        y1_copy(chunk).wait_recv()
        x2_out[chunk] = (keep_x[chunk] + y1_in[chunk, 1].astype(jnp.float32)).astype(jnp.bfloat16)
        x2_copy(chunk).start()
        keep_me[chunk, :, :half] += x1_in[chunk, 0].astype(jnp.float32)
        keep_me[chunk, :, half:] += y1_in[chunk, 0].astype(jnp.float32)

    def normalise(chunk):
        y2_copy(chunk).wait_recv()
        x2_copy(chunk).wait_recv()
        low = keep_me[chunk, :, :half] + y2_in[chunk].astype(jnp.float32)
        high = keep_me[chunk, :, half:] + x2_in[chunk].astype(jnp.float32)
        squares = jnp.sum(low * low, axis=1, keepdims=True) + jnp.sum(
            high * high, axis=1, keepdims=True
        )
        ratio = lax.rsqrt(squares * (1.0 / width) + norm_eps)
        keep_me[chunk, :, :half] = low * ratio * gains_ref[:, :half].astype(jnp.float32)
        keep_me[chunk, :, half:] = high * ratio * gains_ref[:, half:].astype(jnp.float32)

    def hand_on(chunk):
        pltpu.make_async_copy(base.at[chunk], base.at[chunk], chain_sem.at[1, chunk]).wait()
        out_ref[chunk] = (base[chunk].astype(jnp.float32) + keep_me[chunk]).astype(out_ref.dtype)

        @pl.when(section < sections - 1)
        def _():
            chain_copy(chunk).start()

    def turn(ahead, carry):
        step = ahead - LEAD

        @pl.when((ahead % part_chunks == 0) & (ahead < chunks))
        def _():
            attend(ahead // part_chunks)

        @pl.when(step == 0)
        def _():
            w_copy.wait()
            gains_copy.wait()

        for lag, stage in enumerate((for_sibling, first_turn, second_turn, normalise)):
            chunk = step - lag

            @pl.when((chunk >= 0) & (chunk < chunks))
            def _():
                stage(chunk)

        passed = step - 3 - section

        @pl.when((passed >= 0) & (passed < chunks))
        def _():
            hand_on(passed)

        return carry

    lax.fori_loop(0, LEAD + chunks + 3 + sections - 1, turn, 0)

    for wave in exchanges:
        for copy in wave:
            copy.wait_send()

    def finish(chunk, carry):
        for copy in (pair_copy, x1_copy, y1_copy, x2_copy, y2_copy):
            copy(chunk).wait_send()

        @pl.when(section < sections - 1)
        def _():
            chain_copy(chunk).wait_send()

        return carry

    lax.fori_loop(0, chunks, finish, 0)


def by_head(sections, chunks, parts, stream, queries, keys, values, out_weight, gains):
    devices = lax.axis_size("ctx")
    rows, width = stream.shape
    query_width = queries.shape[2] // devices
    chunk_rows = rows // chunks
    half = (width // LANES + 1) // 2 * LANES
    other = width - half
    chips = devices // 2
    narrow, wide = jnp.bfloat16, jnp.float32
    anywhere = pl.BlockSpec(memory_space=pl.ANY)
    in_vmem = pl.BlockSpec(memory_space=pltpu.VMEM)
    dma = pltpu.SemaphoreType.DMA
    out = pl.pallas_call(
        functools.partial(fused_kernel, sections, chunks, parts, half),
        out_shape=jax.ShapeDtypeStruct((chunks, chunk_rows, width), narrow),
        in_specs=[anywhere] * 6,
        out_specs=in_vmem,
        scratch_shapes=[
            pltpu.VMEM((devices, rows, query_width), narrow),
            pltpu.VMEM((devices * rows, HEAD_WIDTH), narrow),
            pltpu.VMEM((devices * rows, HEAD_WIDTH), narrow),
            pltpu.VMEM(out_weight.shape[1:], narrow),
            pltpu.VMEM(gains.shape, narrow),
            pltpu.VMEM((2, chunks, chips, chunk_rows, query_width), narrow),
            pltpu.VMEM((chunks, chips, chunk_rows, width), narrow),
            pltpu.VMEM((chunks, chips, chunk_rows, width), narrow),
            pltpu.VMEM((chunks, 2, chunk_rows, half), narrow),
            pltpu.VMEM((chunks, 2, chunk_rows, half), narrow),
            pltpu.VMEM((chunks, 2, chunk_rows, other), narrow),
            pltpu.VMEM((chunks, 2, chunk_rows, other), narrow),
            pltpu.VMEM((chunks, chunk_rows, other), narrow),
            pltpu.VMEM((chunks, chunk_rows, other), narrow),
            pltpu.VMEM((chunks, chunk_rows, half), narrow),
            pltpu.VMEM((chunks, chunk_rows, half), narrow),
            pltpu.VMEM((chunks, chunk_rows, width), wide),
            pltpu.VMEM((chunks, chunk_rows, other), wide),
            pltpu.VMEM((chunks, chunk_rows, half), wide),
            pltpu.VMEM((chunks, chunk_rows, width), narrow),
            dma((2,)),
            dma((2 + parts, devices)),
            dma((2 + parts, devices)),
            dma((2, chunks)),
            dma((2, chunks)),
            dma((2, chunks)),
            dma((2, chunks)),
            dma((2, chunks)),
            dma((2, chunks)),
        ],
        compiler_params=pltpu.CompilerParams(
            collective_id=0, has_side_effects=True, vmem_limit_bytes=VMEM_GRANT
        ),
    )(gains, stream, queries[0], keys[0], values[0], out_weight[0])
    return out.reshape(1, rows, width)


def fits_by_head(mesh, rows):
    devices = mesh.shape["ctx"]
    return devices == KEY_HEADS and devices * rows <= WINDOW_LENGTH and devices % 8 == 0


def solution(mesh):
    in_specs = (
        P("ctx", None),
        P("section", "ctx", None),
        P("section", "ctx", None),
        P("section", "ctx", None),
        P("section", "ctx", None),
        P("section", None),
    )
    out_specs = P("section", "ctx", None)
    sections = mesh.shape["section"]

    def step(stream, *rest):
        rows = stream.shape[0]
        if fits_by_head(mesh, rows):
            return by_head(sections, CHUNKS, PARTS, stream, *rest)
        return local(stream, *rest)

    return jax.shard_map(step, mesh=mesh, in_specs=in_specs, out_specs=out_specs, check_vma=False)
```

```python
import functools
import math

import jax
import jax.numpy as jnp
from jax import lax
from jax.experimental import pallas as pl
from jax.experimental.pallas import tpu as pltpu
from jax.sharding import PartitionSpec as P

KEY_HEADS = 8
HEAD_WIDTH = 128
WINDOW_LENGTH = 1024
QUERY_SCALAR = 168
QUERY_PER_KEY = 2


norm_eps = 1e-06


def passed_along(block, axis, distance):
    devices = range(lax.axis_size(axis))
    route = [(i - distance, i) for i in devices if i - distance in devices]
    return lax.ppermute(block, axis, route)


def attend_block(query_matrix_rows, key_matrix_rows, value_matrix_rows, allowed, scale_factor):
    scores = (
        jnp.einsum(
            "qhgd,khd->hgqk", query_matrix_rows, key_matrix_rows, preferred_element_type=jnp.float32
        )
        * scale_factor
    )
    scores = jnp.where(allowed, scores, -jnp.inf)
    row_top = jnp.max(scores, axis=-1, keepdims=True)
    exponent = jnp.exp(scores - row_top)
    row_total = jnp.sum(exponent, axis=-1, keepdims=True)
    weights = exponent.astype(jnp.bfloat16)
    mixed_rows = jnp.einsum(
        "hgqk,khd->qhgd", weights, value_matrix_rows, preferred_element_type=jnp.float32
    )
    return mixed_rows / jnp.transpose(row_total, (2, 0, 1, 3))


def local(stream, queries, keys, values, out_weight, gains):
    tok_rows = stream.shape[0]
    span_rows = min(tok_rows, WINDOW_LENGTH)
    hop_count = WINDOW_LENGTH // span_rows
    own_tail = (keys[0, tok_rows - span_rows :], values[0, tok_rows - span_rows :])
    pieces = [
        passed_along((own_tail[0], own_tail[1]), "ctx", distance)
        for distance in range(hop_count, 0, -1)
    ]
    key_matrix_rows = jnp.concatenate([piece_pair[0] for piece_pair in pieces] + [keys[0]], axis=0)
    value_matrix_rows = jnp.concatenate(
        [piece_pair[1] for piece_pair in pieces] + [values[0]], axis=0
    )
    ctx_base = lax.axis_index("ctx") * tok_rows
    query_pos = ctx_base + jnp.arange(tok_rows, dtype=jnp.int32)
    key_pos = ctx_base - WINDOW_LENGTH + jnp.arange(WINDOW_LENGTH + tok_rows, dtype=jnp.int32)
    allowed = (
        (key_pos[None, :] >= 0)
        & (key_pos[None, :] <= query_pos[:, None])
        & (key_pos[None, :] > query_pos[:, None] - WINDOW_LENGTH)
    )
    scale_factor = QUERY_SCALAR ** (-0.5)
    heads_per_block = math.gcd(KEY_HEADS, 4)
    query_width = heads_per_block * QUERY_PER_KEY * HEAD_WIDTH
    key_width = heads_per_block * HEAD_WIDTH
    outputs_list = []
    for query_head_group in range(KEY_HEADS // heads_per_block):
        query_cols = queries[
            0, :, query_head_group * query_width : (query_head_group + 1) * query_width
        ].reshape(tok_rows, heads_per_block, QUERY_PER_KEY, HEAD_WIDTH)
        key_cols = key_matrix_rows[
            :, query_head_group * key_width : (query_head_group + 1) * key_width
        ].reshape(WINDOW_LENGTH + tok_rows, heads_per_block, HEAD_WIDTH)
        value_cols = value_matrix_rows[
            :, query_head_group * key_width : (query_head_group + 1) * key_width
        ].reshape(WINDOW_LENGTH + tok_rows, heads_per_block, HEAD_WIDTH)
        mixed_rows = attend_block(query_cols, key_cols, value_cols, allowed, scale_factor)
        outputs_list.append(mixed_rows.reshape(tok_rows, query_width))
    attended = jnp.concatenate(outputs_list, axis=1).astype(jnp.bfloat16)
    projected = jnp.dot(
        attended,
        lax.all_gather(out_weight[0], "ctx", axis=0, tiled=True),
        preferred_element_type=jnp.float32,
    )
    mean_square = jnp.mean(projected * projected, axis=-1, keepdims=True)
    branch = projected * lax.rsqrt(mean_square + norm_eps) * gains[0].astype(jnp.float32)
    section_index = lax.axis_index("section")
    section_count = lax.axis_size("section")
    running = jnp.where(
        section_index == 0, stream.astype(jnp.float32) + branch, jnp.zeros_like(branch)
    )
    for turn_index in range(section_count - 1):
        arrived = passed_along(running.astype(jnp.bfloat16), "section", 1).astype(running.dtype)
        running = jnp.where(section_index == turn_index + 1, arrived + branch, running)
    return running.astype(jnp.bfloat16)[None]


LANES = 128
MESH = pl.DeviceIdType.MESH
CHUNKS = 8
PARTS = 2
LEAD = 2
VMEM_GRANT = 66_300_000


def column_tiles(start, stop, width):
    return [(at, min(at + width, stop) - at) for at in range(start, stop, width)]


def fused_kernel(
    sections,
    chunks,
    parts,
    half,
    gains_hbm,
    stream_ref,
    q_ref,
    k_ref,
    v_ref,
    w_hbm,
    out_ref,
    qbuf,
    kbuf,
    vbuf,
    w_ref,
    gains_ref,
    att,
    pair_out,
    pair_in,
    x1_out,
    x1_in,
    y1_out,
    y1_in,
    x2_out,
    x2_in,
    y2_out,
    y2_in,
    keep_me,
    keep_x,
    keep_y,
    base,
    local_sem,
    a2a_send,
    a2a_recv,
    pair_sem,
    x1_sem,
    y1_sem,
    x2_sem,
    y2_sem,
    chain_sem,
):
    me = lax.axis_index("ctx")
    section = lax.axis_index("section")
    devices, rows, query_width = qbuf.shape
    width = w_ref.shape[1]
    chunk_rows = rows // chunks
    quarter, pair_count = devices // 4, devices // 2
    core = me % 2
    across = (me // quarter) % 2
    up = me // pair_count
    flips = (1 - 2 * core, quarter * (1 - 2 * across), pair_count * (1 - 2 * up))

    def peer(flip_core, flip_x, flip_y):
        return me + flips[0] * flip_core + flips[1] * flip_x + flips[2] * flip_y

    sibling, beside, above, diagonal = peer(1, 0, 0), peer(0, 1, 0), peer(0, 0, 1), peer(0, 1, 1)
    has_prev = jnp.minimum(section, 1)
    has_next = jnp.minimum(sections - 1 - section, 1)

    def own_rows(buf):
        return buf.at[pl.ds(pl.multiple_of(me * rows, rows), rows)]

    def head_columns(ref, who, span):
        return ref.at[:, pl.ds(pl.multiple_of(who * span, span), span)]

    w_copy = pltpu.make_async_copy(w_hbm, w_ref, local_sem.at[0])
    w_copy.start()
    gains_copy = pltpu.make_async_copy(gains_hbm, gains_ref, local_sem.at[1])
    gains_copy.start()

    @pl.when(section == 0)
    def _():
        for chunk in range(chunks):
            pltpu.make_async_copy(
                stream_ref.at[pl.ds(chunk * chunk_rows, chunk_rows)],
                base.at[chunk],
                chain_sem.at[1, chunk],
            ).start()

    part_rows = rows // parts

    def query_part(who, part):
        source = q_ref.at[
            pl.ds(part * part_rows, part_rows),
            pl.ds(pl.multiple_of(who * query_width, query_width), query_width),
        ]
        return source, qbuf.at[me, pl.ds(part * part_rows, part_rows)]

    def pieces(who):
        return [
            (head_columns(k_ref, who, HEAD_WIDTH), own_rows(kbuf)),
            (head_columns(v_ref, who, HEAD_WIDTH), own_rows(vbuf)),
        ] + [query_part(who, part) for part in range(parts)]

    for which, (source, target) in enumerate(pieces(me)):
        pltpu.make_async_copy(source, target, a2a_recv.at[which, me]).start()

    order = [(0, 1, 1), (1, 1, 1), (0, 1, 0), (0, 0, 1), (1, 1, 0), (1, 0, 1), (1, 0, 0)]
    barrier = pltpu.get_barrier_semaphore()
    for flip in order:
        pl.semaphore_signal(barrier, inc=1, device_id=(section, peer(*flip)), device_id_type=MESH)

    @pl.when(section > 0)
    def _():
        pl.semaphore_signal(barrier, inc=1, device_id=(section - 1, me), device_id_type=MESH)

    @pl.when(section < sections - 1)
    def _():
        pl.semaphore_signal(barrier, inc=1, device_id=(section + 1, me), device_id_type=MESH)

    pl.semaphore_wait(barrier, len(order) + has_prev + has_next)

    def exchange(who):
        return [
            pltpu.make_async_remote_copy(
                src_ref=source,
                dst_ref=target,
                send_sem=a2a_send.at[which, who],
                recv_sem=a2a_recv.at[which, me],
                device_id=(section, who),
                device_id_type=MESH,
            )
            for which, (source, target) in enumerate(pieces(who))
        ]

    exchanges = [exchange(peer(*flip)) for flip in order]
    for wave in zip(*exchanges):
        for copy in wave:
            copy.start()

    def arrive(which, target, block):
        pltpu.make_async_copy(target, target, a2a_recv.at[which, block]).wait()

    factor = QUERY_SCALAR ** (-0.5) * math.log2(math.e)
    group = query_width // HEAD_WIDTH
    part_chunks = chunks // parts

    def attend(part):
        low = pl.multiple_of(part * part_rows, part_rows)
        place = lax.broadcasted_iota(jnp.int32, (group, part_rows, rows), 1) + low
        seen = lax.broadcasted_iota(jnp.int32, (group, part_rows, rows), 2) <= place
        seen = seen.reshape(group * part_rows, rows)
        for block in range(devices):

            @pl.when(part == 0)
            def _():
                arrive(0, kbuf.at[pl.ds(block * rows, rows)], block)
                arrive(1, vbuf.at[pl.ds(block * rows, rows)], block)

            arrive(2 + part, qbuf.at[block, pl.ds(low, part_rows)], block)

        for block in range(devices):
            reach = (block + 1) * rows
            asked = jnp.concatenate(
                [
                    qbuf[block, pl.ds(low, part_rows), head * HEAD_WIDTH : (head + 1) * HEAD_WIDTH]
                    for head in range(group)
                ],
                axis=0,
            )
            scores = lax.dot_general(
                asked,
                kbuf[0:reach],
                (((1,), (1,)), ((), ())),
                preferred_element_type=jnp.float32,
            )
            last = jnp.where(seen, scores[:, block * rows :], -jnp.inf)
            if block:
                scores = jnp.concatenate([scores[:, : block * rows], last], axis=1)
            else:
                scores = last
            top = jnp.max(scores, axis=1, keepdims=True)
            exponent = jnp.exp2((scores - top) * factor)
            total = jnp.sum(exponent, axis=1, keepdims=True)
            mixed = jnp.dot(
                exponent.astype(jnp.bfloat16), vbuf[0:reach], preferred_element_type=jnp.float32
            )
            mixed = (mixed / total).astype(jnp.bfloat16)
            for head in range(group):
                for chunk in range(part_chunks):
                    start = head * part_rows + chunk * chunk_rows
                    att[
                        block % 2,
                        part * part_chunks + chunk,
                        block // 2,
                        :,
                        head * HEAD_WIDTH : (head + 1) * HEAD_WIDTH,
                    ] = mixed[start : start + chunk_rows]

    def remote(source, target, sems, chunk, who):
        return pltpu.make_async_remote_copy(
            src_ref=source.at[chunk],
            dst_ref=target.at[chunk],
            send_sem=sems.at[0, chunk],
            recv_sem=sems.at[1, chunk],
            device_id=who,
            device_id_type=MESH,
        )

    def pair_copy(chunk):
        return remote(pair_out, pair_in, pair_sem, chunk, (section, sibling))

    def x1_copy(chunk):
        return remote(x1_out, x1_in, x1_sem, chunk, (section, beside))

    def y1_copy(chunk):
        return remote(y1_out, y1_in, y1_sem, chunk, (section, above))

    def x2_copy(chunk):
        return remote(x2_out, x2_in, x2_sem, chunk, (section, beside))

    def y2_copy(chunk):
        return remote(y2_out, y2_in, y2_sem, chunk, (section, above))

    def chain_copy(chunk):
        return pltpu.make_async_remote_copy(
            src_ref=out_ref.at[chunk],
            dst_ref=base.at[chunk],
            send_sem=chain_sem.at[0, chunk],
            recv_sem=chain_sem.at[1, chunk],
            device_id=(jnp.minimum(section + 1, sections - 1), me),
            device_id_type=MESH,
        )

    chip_count = pair_count
    places = [who // 2 for who in (beside, diagonal, above, me)]

    def for_sibling(chunk):
        left = att[1 - core, chunk].reshape(chip_count * chunk_rows, query_width)
        for at, span in column_tiles(0, width, 512):
            part = jnp.dot(left, w_ref[:, at : at + span], preferred_element_type=jnp.float32)
            pair_out[chunk, :, :, at : at + span] = part.astype(jnp.bfloat16).reshape(
                chip_count, chunk_rows, span
            )
        pair_copy(chunk).start()

    def first_turn(chunk):
        pair_copy(chunk).wait_recv()
        left = jnp.concatenate([att[core, chunk, place] for place in places], axis=0)

        def summed(at, span):
            part = jnp.dot(left, w_ref[:, at : at + span], preferred_element_type=jnp.float32)
            return [
                part[index * chunk_rows : (index + 1) * chunk_rows]
                + pair_in[chunk, place, :, at : at + span].astype(jnp.float32)
                for index, place in enumerate(places)
            ]

        for at, span in column_tiles(0, half, 512):
            to_beside, to_diagonal, to_above, mine = summed(at, span)
            x1_out[chunk, 0, :, at : at + span] = to_beside.astype(jnp.bfloat16)
            x1_out[chunk, 1, :, at : at + span] = to_diagonal.astype(jnp.bfloat16)
            keep_y[chunk, :, at : at + span] = to_above
            keep_me[chunk, :, at : at + span] = mine
        x1_copy(chunk).start()
        for at, span in column_tiles(half, width, 512):
            to_beside, to_diagonal, to_above, mine = summed(at, span)
            y1_out[chunk, 0, :, at - half : at - half + span] = to_above.astype(jnp.bfloat16)
            y1_out[chunk, 1, :, at - half : at - half + span] = to_diagonal.astype(jnp.bfloat16)
            keep_x[chunk, :, at - half : at - half + span] = to_beside
            keep_me[chunk, :, at : at + span] = mine
        y1_copy(chunk).start()

    def second_turn(chunk):
        x1_copy(chunk).wait_recv()
        y2_out[chunk] = (keep_y[chunk] + x1_in[chunk, 1].astype(jnp.float32)).astype(jnp.bfloat16)
        y2_copy(chunk).start()
        y1_copy(chunk).wait_recv()
        x2_out[chunk] = (keep_x[chunk] + y1_in[chunk, 1].astype(jnp.float32)).astype(jnp.bfloat16)
        x2_copy(chunk).start()
        keep_me[chunk, :, :half] += x1_in[chunk, 0].astype(jnp.float32)
        keep_me[chunk, :, half:] += y1_in[chunk, 0].astype(jnp.float32)

    def normalise(chunk):
        y2_copy(chunk).wait_recv()
        x2_copy(chunk).wait_recv()
        low = keep_me[chunk, :, :half] + y2_in[chunk].astype(jnp.float32)
        high = keep_me[chunk, :, half:] + x2_in[chunk].astype(jnp.float32)
        squares = jnp.sum(low * low, axis=1, keepdims=True) + jnp.sum(
            high * high, axis=1, keepdims=True
        )
        ratio = lax.rsqrt(squares * (1.0 / width) + norm_eps)
        keep_me[chunk, :, :half] = low * ratio * gains_ref[:, :half].astype(jnp.float32)
        keep_me[chunk, :, half:] = high * ratio * gains_ref[:, half:].astype(jnp.float32)

    def hand_on(chunk):
        pltpu.make_async_copy(base.at[chunk], base.at[chunk], chain_sem.at[1, chunk]).wait()
        out_ref[chunk] = (base[chunk].astype(jnp.float32) + keep_me[chunk]).astype(out_ref.dtype)

        @pl.when(section < sections - 1)
        def _():
            chain_copy(chunk).start()

    def turn(ahead, carry):
        step = ahead - LEAD

        @pl.when((ahead % part_chunks == 0) & (ahead < chunks))
        def _():
            attend(ahead // part_chunks)

        @pl.when(step == 0)
        def _():
            w_copy.wait()
            gains_copy.wait()

        for lag, stage in enumerate((for_sibling, first_turn, second_turn, normalise)):
            chunk = step - lag

            @pl.when((chunk >= 0) & (chunk < chunks))
            def _():
                stage(chunk)

        passed = step - 3 - section

        @pl.when((passed >= 0) & (passed < chunks))
        def _():
            hand_on(passed)

        return carry

    lax.fori_loop(0, LEAD + chunks + 3 + sections - 1, turn, 0)

    for wave in exchanges:
        for copy in wave:
            copy.wait_send()

    def finish(chunk, carry):
        for copy in (pair_copy, x1_copy, y1_copy, x2_copy, y2_copy):
            copy(chunk).wait_send()

        @pl.when(section < sections - 1)
        def _():
            chain_copy(chunk).wait_send()

        return carry

    lax.fori_loop(0, chunks, finish, 0)


def by_head(sections, chunks, parts, stream, queries, keys, values, out_weight, gains):
    devices = lax.axis_size("ctx")
    rows, width = stream.shape
    query_width = queries.shape[2] // devices
    chunk_rows = rows // chunks
    half = (width // LANES + 1) // 2 * LANES
    other = width - half
    chips = devices // 2
    narrow, wide = jnp.bfloat16, jnp.float32
    anywhere = pl.BlockSpec(memory_space=pl.ANY)
    in_vmem = pl.BlockSpec(memory_space=pltpu.VMEM)
    dma = pltpu.SemaphoreType.DMA
    out = pl.pallas_call(
        functools.partial(fused_kernel, sections, chunks, parts, half),
        out_shape=jax.ShapeDtypeStruct((chunks, chunk_rows, width), narrow),
        in_specs=[anywhere] * 6,
        out_specs=in_vmem,
        scratch_shapes=[
            pltpu.VMEM((devices, rows, query_width), narrow),
            pltpu.VMEM((devices * rows, HEAD_WIDTH), narrow),
            pltpu.VMEM((devices * rows, HEAD_WIDTH), narrow),
            pltpu.VMEM(out_weight.shape[1:], narrow),
            pltpu.VMEM(gains.shape, narrow),
            pltpu.VMEM((2, chunks, chips, chunk_rows, query_width), narrow),
            pltpu.VMEM((chunks, chips, chunk_rows, width), narrow),
            pltpu.VMEM((chunks, chips, chunk_rows, width), narrow),
            pltpu.VMEM((chunks, 2, chunk_rows, half), narrow),
            pltpu.VMEM((chunks, 2, chunk_rows, half), narrow),
            pltpu.VMEM((chunks, 2, chunk_rows, other), narrow),
            pltpu.VMEM((chunks, 2, chunk_rows, other), narrow),
            pltpu.VMEM((chunks, chunk_rows, other), narrow),
            pltpu.VMEM((chunks, chunk_rows, other), narrow),
            pltpu.VMEM((chunks, chunk_rows, half), narrow),
            pltpu.VMEM((chunks, chunk_rows, half), narrow),
            pltpu.VMEM((chunks, chunk_rows, width), wide),
            pltpu.VMEM((chunks, chunk_rows, other), wide),
            pltpu.VMEM((chunks, chunk_rows, half), wide),
            pltpu.VMEM((chunks, chunk_rows, width), narrow),
            dma((2,)),
            dma((2 + parts, devices)),
            dma((2 + parts, devices)),
            dma((2, chunks)),
            dma((2, chunks)),
            dma((2, chunks)),
            dma((2, chunks)),
            dma((2, chunks)),
            dma((2, chunks)),
        ],
        compiler_params=pltpu.CompilerParams(
            collective_id=0, has_side_effects=True, vmem_limit_bytes=VMEM_GRANT
        ),
    )(gains, stream, queries[0], keys[0], values[0], out_weight[0])
    return out.reshape(1, rows, width)


def fits_by_head(mesh, rows):
    devices = mesh.shape["ctx"]
    return devices == KEY_HEADS and devices * rows <= WINDOW_LENGTH and devices % 8 == 0


def solution(mesh):
    in_specs = (
        P("ctx", None),
        P("section", "ctx", None),
        P("section", "ctx", None),
        P("section", "ctx", None),
        P("section", "ctx", None),
        P("section", None),
    )
    out_specs = P("section", "ctx", None)
    sections = mesh.shape["section"]

    def step(stream, *rest):
        rows = stream.shape[0]
        if fits_by_head(mesh, rows):
            return by_head(sections, CHUNKS, PARTS, stream, *rest)
        return local(stream, *rest)

    return jax.shard_map(step, mesh=mesh, in_specs=in_specs, out_specs=out_specs, check_vma=False)
```
